32 devices in a mesh: los: 8 (over z, x), sky: 4 (over y, core).
Axes of the slice: x: 2, y: 2, z: 4, core: 2. Of those that a mesh axis runs over, the one named last changes fastest.
Arguments:
- potentials: bfloat16 [32, 64, 4096], P('los', 'sky'), may hold values from -6 to 6
- shell_weight: float32 [32], P('los'), may hold values from 0.004 to 0.02
- shell_dist: float32 [32], P('los'), may hold values from 1 to 2.28, as said below
- source_dist: float32 [32], P('los'), may hold values from 1 to 2.28, as said below
Outputs:
- convergence: bfloat16 [32, 64, 4096], P('los', 'sky')
- shear_one: bfloat16 [32, 64, 4096], P('los', 'sky')
- shear_two: bfloat16 [32, 64, 4096], P('los', 'sky')
The draws below stay inside these ranges and needn't reach their ends.
Inputs may be any that keep to these rules, and one draw needn't show every extreme that they name: shell_dist rises strictly with the shell index. source_dist[s] lies strictly between shell_dist[s] and shell_dist[s + 1].
All inputs are finite; a program needn't handle non-finite values.
Results may differ from the reference program's by a relative error of at most 0.001.
Values may be sent and summed in bfloat16 or wider, within the bound.
A program may use at most 64 MiB of HBM per device.

```python
import math
import jax
import jax.numpy as jnp
from jax import lax

NCOLS = 4096
SHELLS = 32
NROWS = 64


def distances(key):
    steps = jax.random.uniform(jax.random.fold_in(key, 11), (SHELLS,), jnp.float32, 0.01, 0.04)
    shells = 1.0 + jnp.cumsum(steps) - steps
    gaps = jax.random.uniform(jax.random.fold_in(key, 12), (SHELLS,), jnp.float32, 0.3, 0.9) * steps
    return (shells, shells + gaps)


def draw_shell_dist(key, part):
    return distances(key)[0]


def draw_source_dist(key, part):
    return distances(key)[1]


def steps_of(rng, extent, cuts, low, high):
    def one(dim, blocks):
        draws = jax.random.uniform(jax.random.fold_in(jax.random.fold_in(rng, 6), dim), (blocks,), jnp.float32, low / len(cuts), high / len(cuts))
        return jnp.repeat(jnp.exp(draws), extent[dim] // blocks).reshape((-1,) + (1,) * (len(extent) - dim - 1))

    level = one(*cuts[0])
    for cut in cuts[1:]:
        level = level * one(*cut)
    return level


def gaussian(stream_key, dims, deviation, most, shards=(), kind=jnp.bfloat16):
    entries = jax.random.normal(stream_key, dims, jnp.float32) * deviation
    if len(shards) > 0:
        entries = steps_of(stream_key, dims, shards, -0.22, 0.18) * entries
    return jnp.clip(entries, min=-most, max=most).astype(kind)


def setup_inputs(seed: int = 0) -> dict:
    streams_of = jax.random.split(jax.random.key(seed), 5)
    potentials = gaussian(streams_of[0], (SHELLS, NROWS, NCOLS), 1.0, 6.0, ((0, 8), (1, 4)))
    shell_weight = jnp.clip(jnp.exp(math.log(0.02) - 1.6094378 * jax.random.uniform(streams_of[1], (SHELLS,), jnp.float32) ** steps_of(streams_of[1], (SHELLS,), ((0, 8),), -0.2, 0.2)), 0.004, 0.02)
    shell_dist = draw_shell_dist(jax.random.fold_in(streams_of[4], 71), 0)
    source_dist = draw_source_dist(jax.random.fold_in(streams_of[4], 71), 0)
    return dict(potentials=potentials, shell_weight=shell_weight, shell_dist=shell_dist, source_dist=source_dist)


def first_diff(field, axis):
    return (jnp.roll(field, 2, axis=axis) - 8.0 * jnp.roll(field, 1, axis=axis) + 8.0 * jnp.roll(field, -1, axis=axis) - jnp.roll(field, -2, axis=axis)) / 12.0


def second_diff(field, axis):
    return (-jnp.roll(field, 2, axis=axis) + 16.0 * jnp.roll(field, 1, axis=axis) - 30.0 * field + 16.0 * jnp.roll(field, -1, axis=axis) - jnp.roll(field, -2, axis=axis)) / 12.0


def reference(potentials, shell_weight, shell_dist, source_dist):
    near_weight = shell_weight * shell_dist
    far_weight = near_weight * shell_dist
    start = jnp.zeros((potentials.shape[1], potentials.shape[2]), jnp.float32)

    def advance(carry, items):
        running_near, running_far = carry
        potential, near_one, far_one, source_one = items
        field = potential.astype(jnp.float32)
        running_near = running_near + near_one * field
        running_far = running_far + far_one * field
        lens_map = running_near - running_far / source_one
        second_x = second_diff(lens_map, 1)
        second_y = second_diff(lens_map, 0)
        cross = first_diff(first_diff(lens_map, 1), 0)
        convergence = (0.5 * (second_x + second_y)).astype(jnp.bfloat16)
        shear_one = (0.5 * (second_x - second_y)).astype(jnp.bfloat16)
        shear_two = cross.astype(jnp.bfloat16)
        return (running_near, running_far), (convergence, shear_one, shear_two)

    carry, outputs = lax.scan(advance, (start, start), (potentials, near_weight, far_weight, source_dist))
    return outputs[0], outputs[1], outputs[2]
```

```python
import functools

import jax
import jax.numpy as jnp
from jax import lax
from jax.experimental import pallas as pl
from jax.experimental.pallas import tpu as pltpu
from jax.sharding import PartitionSpec as P

MESH = pl.DeviceIdType.MESH


def lens_kernel(
    los, sky, chunks, width, weight_ref, dist_ref, source_ref, pot_hbm,
    conv_ref, one_ref, two_ref,
    pot, edge_send, edge_recv, sent, own, got, sent_rim, own_rim, got_rim,
    before, before_rim, onward, onward_rim, back, back_rim,
    prefix, prefix_rim, rim_pot, lens,
    load_sem, edge_ssem, edge_rsem, x_ssem, x_rsem, z_ssem, z_rsem, b_ssem, b_rsem,
):
    f32 = jnp.float32
    shells, rows = pot.shape[0], pot.shape[1]
    half = chunks * width
    me = lax.axis_index("los")
    strip = lax.axis_index("sky")
    q = me // 2
    r = me % 2
    last = los // 2 - 1
    partner = me + 1 - 2 * r
    up = (strip + sky - 1) % sky
    down = (strip + 1) % sky

    load = pltpu.make_async_copy(pot_hbm, pot, load_sem)
    load.start()

    barrier = pltpu.get_barrier_semaphore()
    pl.semaphore_signal(barrier, inc=1, device_id={"los": partner}, device_id_type=MESH)
    pl.semaphore_signal(barrier, inc=1, device_id={"sky": up}, device_id_type=MESH)
    pl.semaphore_signal(barrier, inc=1, device_id={"sky": down}, device_id_type=MESH)

    @pl.when(q > 0)
    def _():
        pl.semaphore_signal(barrier, inc=1, device_id={"los": me - 2}, device_id_type=MESH)

    @pl.when(q < last)
    def _():
        pl.semaphore_signal(barrier, inc=1, device_id={"los": me + 2}, device_id_type=MESH)

    near = [weight_ref[j] * dist_ref[j] for j in range(shells)]
    far = [near[j] * dist_ref[j] for j in range(shells)]
    row = lax.broadcasted_iota(jnp.int32, (8, width), 0)

    load.wait()

    span = 2 * chunks
    for k in range(span):
        cols = pl.ds(k * width, width)
        top = jnp.zeros((8, width), f32)
        bottom = jnp.zeros((8, width), f32)
        for j in range(shells):
            block = pot[j, :, cols].astype(f32)
            mine = (row >= 2 * j) & (row < 2 * j + 2)
            head = block[:8]
            tail = block[rows - 8 :]
            top = jnp.where(mine, pltpu.roll(head, (2 * j) % 8, 0), top)
            bottom = jnp.where(mine, pltpu.roll(tail, (2 * j + 2) % 8, 0), bottom)
        edge_send[0, :, cols] = top.astype(jnp.bfloat16)
        edge_send[1, :, cols] = bottom.astype(jnp.bfloat16)

    peers = 3 + (q > 0).astype(jnp.int32) + (q < last).astype(jnp.int32)
    pl.semaphore_wait(barrier, peers)

    def remote(src, dst, ssem, rsem, **where):
        return pltpu.make_async_remote_copy(
            src_ref=src, dst_ref=dst, send_sem=ssem, recv_sem=rsem,
            device_id=where, device_id_type=MESH,
        )

    edges = [
        remote(edge_send.at[0], edge_recv.at[0], edge_ssem.at[0], edge_rsem.at[0], sky=up),
        remote(edge_send.at[1], edge_recv.at[1], edge_ssem.at[1], edge_rsem.at[1], sky=down),
    ]
    for copy in edges:
        copy.start()

    def totals(start):
        cols = pl.ds(pl.multiple_of(start, 128), width)
        total_near = jnp.zeros((rows, width), f32)
        total_far = jnp.zeros((rows, width), f32)
        for j in range(shells):
            block = pot[j, :, cols].astype(f32)
            total_near = total_near + near[j] * block
            total_far = total_far + far[j] * block
        return jnp.concatenate([total_near, total_far], axis=0)

    x_copies = [
        remote(sent.at[c], got.at[c], x_ssem.at[c], x_rsem.at[c], los=partner)
        for c in range(chunks)
    ] + [remote(sent_rim, got_rim, x_ssem.at[chunks], x_rsem.at[chunks], los=partner)]
    z_copies = [
        remote(onward.at[c], before.at[c], z_ssem.at[c], z_rsem.at[c], los=me + 2)
        for c in range(chunks)
    ] + [remote(onward_rim, before_rim, z_ssem.at[chunks], z_rsem.at[chunks], los=me + 2)]
    b_copies = [
        remote(back.at[c], prefix.at[r, c], b_ssem.at[c], b_rsem.at[c], los=partner)
        for c in range(chunks)
    ] + [remote(back_rim, prefix_rim.at[r], b_ssem.at[chunks], b_rsem.at[chunks], los=partner)]

    for c in range(chunks):
        sent[c] = totals((1 - r) * half + c * width)
        x_copies[c].start()
    for c in range(chunks):
        own[c] = totals(r * half + c * width)

    @pl.when(q == 0)
    def _():
        before[...] = jnp.zeros(before.shape, f32)
        before_rim[...] = jnp.zeros(before_rim.shape, f32)

    for copy in edges:
        copy.wait_recv()

    inner = (row >= 2) & (row < 6)
    for k in range(span):
        cols = pl.ds(k * width, width)
        below = edge_recv[0, :, cols].astype(f32)
        above = edge_recv[1, :, cols].astype(f32)
        total = jnp.zeros((8, width), f32)
        for j in range(shells):
            tile = jnp.where(
                row < 2,
                pltpu.roll(below, (8 - 2 * j) % 8, 0),
                jnp.where(
                    row < 4,
                    pltpu.roll(below, (10 - 2 * j) % 8, 0),
                    jnp.where(
                        row < 6,
                        pltpu.roll(above, (12 - 2 * j) % 8, 0),
                        pltpu.roll(above, (14 - 2 * j) % 8, 0),
                    ),
                ),
            )
            scaled = tile * jnp.where(inner, far[j], near[j])
            rim_pot[j, k] = scaled
            total = total + scaled
        own_rim[k // chunks, k % chunks] = total
    sent_rim[...] = own_rim[1 - r]
    x_copies[chunks].start()

    is_odd = r.astype(f32)
    is_even = 1.0 - is_odd

    for c in range(chunks + 1):
        x_copies[c].wait_recv()

        @pl.when(q > 0)
        def _():
            z_copies[c].wait_recv()

        if c < chunks:
            mine, other, base = own[c], got[c], before[c]
            next_ref, back_ref, keep_ref = onward.at[c], back.at[c], prefix.at[r, c]
        else:
            mine, other, base = own_rim[r], got_rim[...], before_rim[...]
            next_ref, back_ref, keep_ref = onward_rim, back_rim, prefix_rim.at[r]
        next_ref[...] = base + (mine + other)

        @pl.when(q < last)
        def _():
            z_copies[c].start()

        back_ref[...] = base + is_even * mine
        b_copies[c].start()
        keep_ref[...] = base + is_odd * other

    for c in range(chunks + 1):
        b_copies[c].wait_recv()

    inverse = [1.0 / jnp.full((8, width), source_ref[j], f32) for j in range(shells)]

    def lens_chunk(k, carry):
        cols = pl.ds(pl.multiple_of(k * width, 128), width)
        part, c = k // chunks, k % chunks
        sums = prefix[part, c]
        run_near, run_far = sums[:rows], sums[rows:]
        rim = prefix_rim[part, c]
        for j in range(shells):
            block = pot[j, :, cols].astype(f32)
            run_near = run_near + near[j] * block
            run_far = run_far + far[j] * block
            rim = rim + rim_pot[j, k]
            far_rim = jnp.where(row < 4, pltpu.roll(rim, 6, 0), pltpu.roll(rim, 2, 0))
            scale = jnp.concatenate([inverse[j]] * (rows // 8), axis=0)
            lens[j, k, :rows] = run_near - run_far * scale
            lens[j, k, rows:] = rim - far_rim * inverse[j]
        return carry

    lax.fori_loop(0, span, lens_chunk, 0)

    def stencil_chunk(k, carry):
        cols = pl.ds(pl.multiple_of(k * width, 128), width)
        before_k = (k + span - 1) % span
        after_k = (k + 1) % span
        for j in range(shells):
            centre = lens[j, k]
            wide = jnp.concatenate(
                [lens[j, before_k, :, width - 128 :], centre, lens[j, after_k, :, :128]], axis=1
            )
            full = width + 256

            def shift(n):
                return pltpu.roll(wide, n % full, 1)[:, 128 : 128 + width]

            left1, right1, left2, right2 = shift(1), shift(-1), shift(2), shift(-2)
            slope = (left2 - right2) + 8.0 * (right1 - left1)
            second_x = (16.0 * (left1 + right1) - (left2 + right2))[:rows]

            def rows_at(field, n):
                return pltpu.roll(field, (-n) % (rows + 8), 0)[:rows]

            second_y = 16.0 * (rows_at(centre, -1) + rows_at(centre, 1)) - (
                rows_at(centre, -2) + rows_at(centre, 2)
            )
            cross = (rows_at(slope, -2) - rows_at(slope, 2)) + 8.0 * (
                rows_at(slope, 1) - rows_at(slope, -1)
            )
            middle = 60.0 * centre[:rows]
            conv_ref[j, :, cols] = ((second_x + second_y - middle) * (1.0 / 24.0)).astype(jnp.bfloat16)
            one_ref[j, :, cols] = ((second_x - second_y) * (1.0 / 24.0)).astype(jnp.bfloat16)
            two_ref[j, :, cols] = (cross * (1.0 / 144.0)).astype(jnp.bfloat16)
        return carry

    lax.fori_loop(0, span, stencil_chunk, 0)

    for copy in edges:
        copy.wait_send()
    for c in range(chunks + 1):
        x_copies[c].wait_send()
        b_copies[c].wait_send()

    @pl.when(q < last)
    def _():
        for c in range(chunks + 1):
            z_copies[c].wait_send()


def on_device(los, sky, potentials, shell_weight, shell_dist, source_dist):
    shells, rows, ncols = potentials.shape
    half = ncols // 2
    chunks = next(n for n in (8, 4, 2, 1) if half % (n * 128) == 0)
    width = half // chunks
    f32, bf16 = jnp.float32, jnp.bfloat16
    dma = pltpu.SemaphoreType.DMA
    smem = pl.BlockSpec(memory_space=pltpu.SMEM)
    vmem = pl.BlockSpec(memory_space=pltpu.VMEM)
    main = (chunks, 2 * rows, width)
    rim = (chunks, 8, width)
    return tuple(pl.pallas_call(
        functools.partial(lens_kernel, los, sky, chunks, width),
        out_shape=[jax.ShapeDtypeStruct(potentials.shape, bf16)] * 3,
        in_specs=[smem, smem, smem, pl.BlockSpec(memory_space=pl.ANY)],
        out_specs=[vmem] * 3,
        scratch_shapes=[
            pltpu.VMEM(potentials.shape, bf16),
            pltpu.VMEM((2, 8, ncols), bf16),
            pltpu.VMEM((2, 8, ncols), bf16),
            pltpu.VMEM(main, f32),
            pltpu.VMEM(main, f32),
            pltpu.VMEM(main, f32),
            pltpu.VMEM(rim, f32),
            pltpu.VMEM((2,) + rim, f32),
            pltpu.VMEM(rim, f32),
            pltpu.VMEM(main, f32),
            pltpu.VMEM(rim, f32),
            pltpu.VMEM(main, f32),
            pltpu.VMEM(rim, f32),
            pltpu.VMEM(main, f32),
            pltpu.VMEM(rim, f32),
            pltpu.VMEM((2,) + main, f32),
            pltpu.VMEM((2,) + rim, f32),
            pltpu.VMEM((shells, 2 * chunks, 8, width), f32),
            pltpu.VMEM((shells, 2 * chunks, rows + 8, width), f32),
            dma,
            dma((2,)),
            dma((2,)),
            dma((chunks + 1,)),
            dma((chunks + 1,)),
            dma((chunks + 1,)),
            dma((chunks + 1,)),
            dma((chunks + 1,)),
            dma((chunks + 1,)),
        ],
        compiler_params=pltpu.CompilerParams(collective_id=0, has_side_effects=True),
    )(shell_weight, shell_dist, source_dist, potentials))


def solution(mesh):
    return jax.shard_map(
        functools.partial(on_device, mesh.shape["los"], mesh.shape["sky"]),
        mesh=mesh,
        in_specs=(P("los", "sky", None), P("los"), P("los"), P("los")),
        out_specs=(P("los", "sky", None), P("los", "sky", None), P("los", "sky", None)),
        check_vma=False,
    )
```

```python
import functools

import jax
import jax.numpy as jnp
from jax import lax
from jax.experimental import pallas as pl
from jax.experimental.pallas import tpu as pltpu
from jax.sharding import PartitionSpec as P

MESH = pl.DeviceIdType.MESH


def lens_kernel(
    los, sky, chunks, width, weight_ref, dist_ref, source_ref, pot_hbm,
    conv_ref, one_ref, two_ref,
    pot, edge_send, edge_recv, sent, own, got, sent_rim, own_rim, got_rim,
    before, before_rim, onward, onward_rim, back, back_rim,
    prefix, prefix_rim, rim_pot, lens,
    load_sem, edge_ssem, edge_rsem, x_ssem, x_rsem, z_ssem, z_rsem, b_ssem, b_rsem,
):
    f32 = jnp.float32
    shells, rows = pot.shape[0], pot.shape[1]
    half = chunks * width
    me = lax.axis_index("los")
    strip = lax.axis_index("sky")
    q = me // 2
    r = me % 2
    last = los // 2 - 1
    partner = me + 1 - 2 * r
    up = (strip + sky - 1) % sky
    down = (strip + 1) % sky

    span = 2 * chunks
    loads = []
    for c in range(span):
        part = (1 - r) if c < chunks else r
        cols = pl.ds(pl.multiple_of((part * chunks + c % chunks) * width, 128), width)
        loads.append(
            pltpu.make_async_copy(pot_hbm.at[:, :, cols], pot.at[:, :, cols], load_sem.at[c])
        )
        loads[-1].start()

    barrier = pltpu.get_barrier_semaphore()
    pl.semaphore_signal(barrier, inc=1, device_id={"los": partner}, device_id_type=MESH)
    pl.semaphore_signal(barrier, inc=1, device_id={"sky": up}, device_id_type=MESH)
    pl.semaphore_signal(barrier, inc=1, device_id={"sky": down}, device_id_type=MESH)

    @pl.when(q > 0)
    def _():
        pl.semaphore_signal(barrier, inc=1, device_id={"los": me - 2}, device_id_type=MESH)

    @pl.when(q < last)
    def _():
        pl.semaphore_signal(barrier, inc=1, device_id={"los": me + 2}, device_id_type=MESH)

    near = [weight_ref[j] * dist_ref[j] for j in range(shells)]
    far = [near[j] * dist_ref[j] for j in range(shells)]
    row = lax.broadcasted_iota(jnp.int32, (8, width), 0)

    def totals(start):
        cols = pl.ds(pl.multiple_of(start, 128), width)
        total_near = jnp.zeros((rows, width), f32)
        total_far = jnp.zeros((rows, width), f32)
        for j in range(shells):
            block = pot[j, :, cols].astype(f32)
            total_near = total_near + near[j] * block
            total_far = total_far + far[j] * block
        return jnp.concatenate([total_near, total_far], axis=0)

    def remote(src, dst, ssem, rsem, **where):
        return pltpu.make_async_remote_copy(
            src_ref=src, dst_ref=dst, send_sem=ssem, recv_sem=rsem,
            device_id=where, device_id_type=MESH,
        )

    x_copies = [
        remote(sent.at[c], got.at[c], x_ssem.at[c], x_rsem.at[c], los=partner)
        for c in range(chunks)
    ] + [remote(sent_rim, got_rim, x_ssem.at[chunks], x_rsem.at[chunks], los=partner)]
    z_copies = [
        remote(onward.at[c], before.at[c], z_ssem.at[c], z_rsem.at[c], los=me + 2)
        for c in range(chunks)
    ] + [remote(onward_rim, before_rim, z_ssem.at[chunks], z_rsem.at[chunks], los=me + 2)]
    b_copies = [
        remote(back.at[c], prefix.at[r, c], b_ssem.at[c], b_rsem.at[c], los=partner)
        for c in range(chunks)
    ] + [remote(back_rim, prefix_rim.at[r], b_ssem.at[chunks], b_rsem.at[chunks], los=partner)]

    edges = [
        remote(edge_send.at[0], edge_recv.at[0], edge_ssem.at[0], edge_rsem.at[0], sky=up),
        remote(edge_send.at[1], edge_recv.at[1], edge_ssem.at[1], edge_rsem.at[1], sky=down),
    ]
    rim_at = max(1, chunks * 5 // 8)

    def send_totals(c):
        sent[c] = totals((1 - r) * half + c * width)
        x_copies[c].start()

    loads[0].wait()
    sent[0] = totals((1 - r) * half)

    peers = 3 + (q > 0).astype(jnp.int32) + (q < last).astype(jnp.int32)
    pl.semaphore_wait(barrier, peers)

    x_copies[0].start()
    for copy in loads[1:]:
        copy.wait()

    for k in range(span):
        cols = pl.ds(k * width, width)
        top = jnp.zeros((8, width), f32)
        bottom = jnp.zeros((8, width), f32)
        for j in range(shells):
            block = pot[j, :, cols].astype(f32)
            mine = (row >= 2 * j) & (row < 2 * j + 2)
            head = block[:8]
            tail = block[rows - 8 :]
            top = jnp.where(mine, pltpu.roll(head, (2 * j) % 8, 0), top)
            bottom = jnp.where(mine, pltpu.roll(tail, (2 * j + 2) % 8, 0), bottom)
        edge_send[0, :, cols] = top.astype(jnp.bfloat16)
        edge_send[1, :, cols] = bottom.astype(jnp.bfloat16)

    for copy in edges:
        copy.start()
    for c in range(1, rim_at):
        send_totals(c)
    for c in range(chunks):
        own[c] = totals(r * half + c * width)

    @pl.when(q == 0)
    def _():
        before[...] = jnp.zeros(before.shape, f32)
        before_rim[...] = jnp.zeros(before_rim.shape, f32)

    for copy in edges:
        copy.wait_recv()

    inner = (row >= 2) & (row < 6)
    for k in range(span):
        cols = pl.ds(k * width, width)
        below = edge_recv[0, :, cols].astype(f32)
        above = edge_recv[1, :, cols].astype(f32)
        total = jnp.zeros((8, width), f32)
        for j in range(shells):
            tile = jnp.where(
                row < 2,
                pltpu.roll(below, (8 - 2 * j) % 8, 0),
                jnp.where(
                    row < 4,
                    pltpu.roll(below, (10 - 2 * j) % 8, 0),
                    jnp.where(
                        row < 6,
                        pltpu.roll(above, (12 - 2 * j) % 8, 0),
                        pltpu.roll(above, (14 - 2 * j) % 8, 0),
                    ),
                ),
            )
            scaled = tile * jnp.where(inner, far[j], near[j])
            rim_pot[j, k] = scaled
            total = total + scaled
        own_rim[k // chunks, k % chunks] = total
    sent_rim[...] = own_rim[1 - r]
    x_copies[chunks].start()

    for c in range(rim_at, chunks):
        send_totals(c)

    is_odd = r.astype(f32)
    is_even = 1.0 - is_odd

    def forward(c):
        x_copies[c].wait_recv()

        @pl.when(q > 0)
        def _():
            z_copies[c].wait_recv()

        if c < chunks:
            mine, other, base = own[c], got[c], before[c]
            next_ref, back_ref, keep_ref = onward.at[c], back.at[c], prefix.at[r, c]
        else:
            mine, other, base = own_rim[r], got_rim[...], before_rim[...]
            next_ref, back_ref, keep_ref = onward_rim, back_rim, prefix_rim.at[r]
        next_ref[...] = base + (mine + other)

        @pl.when(q < last)
        def _():
            z_copies[c].start()

        back_ref[...] = base + is_even * mine
        b_copies[c].start()
        keep_ref[...] = base + is_odd * other

    inverse = [1.0 / jnp.full((8, width), source_ref[j], f32) for j in range(shells)]

    def lens_chunk(place, carry):
        k = (r * chunks + place) % span
        cols = pl.ds(pl.multiple_of(k * width, 128), width)
        part, c = k // chunks, k % chunks
        sums = prefix[part, c]
        run_near, run_far = sums[:rows], sums[rows:]
        rim = prefix_rim[part, c]
        for j in range(shells):
            block = pot[j, :, cols].astype(f32)
            run_near = run_near + near[j] * block
            run_far = run_far + far[j] * block
            rim = rim + rim_pot[j, k]
            far_rim = jnp.where(row < 4, pltpu.roll(rim, 6, 0), pltpu.roll(rim, 2, 0))
            scale = jnp.concatenate([inverse[j]] * (rows // 8), axis=0)
            lens[j, k, :rows] = run_near - run_far * scale
            lens[j, k, rows:] = rim - far_rim * inverse[j]
        return carry

    def stencil_chunk(place, carry):
        k = (r * chunks + place) % span
        cols = pl.ds(pl.multiple_of(k * width, 128), width)
        before_k = (k + span - 1) % span
        after_k = (k + 1) % span
        for j in range(shells):
            centre = lens[j, k]
            wide = jnp.concatenate(
                [lens[j, before_k, :, width - 128 :], centre, lens[j, after_k, :, :128]], axis=1
            )
            full = width + 256

            def shift(n):
                return pltpu.roll(wide, n % full, 1)[:, 128 : 128 + width]

            left1, right1, left2, right2 = shift(1), shift(-1), shift(2), shift(-2)
            slope = (left2 - right2) + 8.0 * (right1 - left1)
            second_x = (16.0 * (left1 + right1) - (left2 + right2))[:rows]

            def rows_at(field, n):
                return pltpu.roll(field, (-n) % (rows + 8), 0)[:rows]

            second_y = 16.0 * (rows_at(centre, -1) + rows_at(centre, 1)) - (
                rows_at(centre, -2) + rows_at(centre, 2)
            )
            cross = (rows_at(slope, -2) - rows_at(slope, 2)) + 8.0 * (
                rows_at(slope, 1) - rows_at(slope, -1)
            )
            middle = 60.0 * centre[:rows]
            conv_ref[j, :, cols] = ((second_x + second_y - middle) * (1.0 / 24.0)).astype(jnp.bfloat16)
            one_ref[j, :, cols] = ((second_x - second_y) * (1.0 / 24.0)).astype(jnp.bfloat16)
            two_ref[j, :, cols] = (cross * (1.0 / 144.0)).astype(jnp.bfloat16)
        return carry

    order = list(range(rim_at)) + [chunks] + list(range(rim_at, chunks))

    @pl.when(q < last)
    def _():
        for c in order:
            forward(c)
        lax.fori_loop(0, chunks, lens_chunk, 0)
        lax.fori_loop(1, chunks - 1, stencil_chunk, 0)
        for c in order:
            b_copies[c].wait_recv()
        lax.fori_loop(chunks, span, lens_chunk, 0)
        lax.fori_loop(chunks - 1, span + 1, stencil_chunk, 0)

    @pl.when(q == last)
    def _():
        arrived, mapped, done = set(), set(), set()

        def run(body, places):
            while places:
                count = 1
                while count < len(places) and places[count] == places[0] + count:
                    count += 1
                lax.fori_loop(places[0], places[0] + count, body, 0)
                places = places[count:]

        def advance(limit):
            ready = []
            for place in sorted(arrived - mapped):
                rim_place = "own" if place < chunks else "other"
                if rim_place in rims:
                    ready.append(place)
            run(lens_chunk, ready)
            mapped.update(ready)
            ready = [
                place
                for place in range(span)
                if place not in done
                and {(place - 1) % span, place, (place + 1) % span} <= mapped
            ][:limit]
            run(stencil_chunk, ready)
            done.update(ready)

        rims = set()

        def receive(c):
            b_copies[c].wait_recv()
            if c == chunks:
                rims.add("other")
            else:
                arrived.add(chunks + c)

        waited = 0
        for n, c in enumerate(order):
            forward(c)
            if c == chunks:
                rims.add("own")
            else:
                arrived.add(c)
            if "own" in rims and n > rim_at:
                while waited < n - 1:
                    receive(order[waited])
                    waited += 1
            advance(4)
        for c in order[waited:]:
            receive(c)
            advance(span)

    for copy in edges:
        copy.wait_send()
    for c in range(chunks + 1):
        x_copies[c].wait_send()
        b_copies[c].wait_send()

    @pl.when(q < last)
    def _():
        for c in range(chunks + 1):
            z_copies[c].wait_send()


def store_kernel(a, b, c, to_a, to_b, to_c, sems):
    copies = [
        pltpu.make_async_copy(src.at[j], dst.at[j], sems.at[n, j])
        for n, (src, dst) in enumerate(((a, to_a), (b, to_b), (c, to_c)))
        for j in range(a.shape[0])
    ]
    for copy in copies:
        copy.start()
    for copy in copies:
        copy.wait()


def on_device(los, sky, potentials, shell_weight, shell_dist, source_dist):
    shells, rows, ncols = potentials.shape
    half = ncols // 2
    chunks = next(n for n in (8, 4, 2, 1) if half % (n * 128) == 0)
    width = half // chunks
    f32, bf16 = jnp.float32, jnp.bfloat16
    dma = pltpu.SemaphoreType.DMA
    smem = pl.BlockSpec(memory_space=pltpu.SMEM)
    vmem = pl.BlockSpec(memory_space=pltpu.VMEM)
    main = (chunks, 2 * rows, width)
    rim = (chunks, 8, width)
    staged = pl.pallas_call(
        functools.partial(lens_kernel, los, sky, chunks, width),
        out_shape=[pltpu.VMEM(potentials.shape, bf16)] * 3,
        in_specs=[smem, smem, smem, pl.BlockSpec(memory_space=pl.ANY)],
        out_specs=[vmem] * 3,
        scratch_shapes=[
            pltpu.VMEM(potentials.shape, bf16),
            pltpu.VMEM((2, 8, ncols), bf16),
            pltpu.VMEM((2, 8, ncols), bf16),
            pltpu.VMEM(main, f32),
            pltpu.VMEM(main, f32),
            pltpu.VMEM(main, f32),
            pltpu.VMEM(rim, f32),
            pltpu.VMEM((2,) + rim, f32),
            pltpu.VMEM(rim, f32),
            pltpu.VMEM(main, f32),
            pltpu.VMEM(rim, f32),
            pltpu.VMEM(main, f32),
            pltpu.VMEM(rim, f32),
            pltpu.VMEM(main, f32),
            pltpu.VMEM(rim, f32),
            pltpu.VMEM((2,) + main, f32),
            pltpu.VMEM((2,) + rim, f32),
            pltpu.VMEM((shells, 2 * chunks, 8, width), f32),
            pltpu.VMEM((shells, 2 * chunks, rows + 8, width), f32),
            dma((2 * chunks,)),
            dma((2,)),
            dma((2,)),
            dma((chunks + 1,)),
            dma((chunks + 1,)),
            dma((chunks + 1,)),
            dma((chunks + 1,)),
            dma((chunks + 1,)),
            dma((chunks + 1,)),
        ],
        compiler_params=pltpu.CompilerParams(collective_id=0, has_side_effects=True),
    )(shell_weight, shell_dist, source_dist, potentials)
    anywhere = pl.BlockSpec(memory_space=pl.ANY)
    return tuple(pl.pallas_call(
        store_kernel,
        out_shape=[jax.ShapeDtypeStruct(potentials.shape, bf16)] * 3,
        in_specs=[vmem] * 3,
        out_specs=[anywhere] * 3,
        scratch_shapes=[dma((3, shells))],
    )(*[pltpu.with_memory_space_constraint(x, pltpu.VMEM) for x in staged]))


def solution(mesh):
    return jax.shard_map(
        functools.partial(on_device, mesh.shape["los"], mesh.shape["sky"]),
        mesh=mesh,
        in_specs=(P("los", "sky", None), P("los"), P("los"), P("los")),
        out_specs=(P("los", "sky", None), P("los", "sky", None), P("los", "sky", None)),
        check_vma=False,
    )
```

```python
import functools

import jax
import jax.numpy as jnp
from jax import lax
from jax.experimental import pallas as pl
from jax.experimental.pallas import tpu as pltpu
from jax.sharding import PartitionSpec as P

MESH = pl.DeviceIdType.MESH


def lens_kernel(
    los, sky, chunks, width, weight_ref, dist_ref, source_ref, pot_hbm,
    conv_ref, one_ref, two_ref,
    pot, edge_send, edge_recv, sent, own, got, sent_rim, own_rim, got_rim,
    before, before_rim, onward, onward_rim, back, back_rim,
    prefix, prefix_rim, rim_pot, lens,
    load_sem, edge_ssem, edge_rsem, x_ssem, x_rsem, z_ssem, z_rsem, b_ssem, b_rsem,
):
    f32 = jnp.float32
    shells, rows = pot.shape[0], pot.shape[1]
    half = chunks * width
    me = lax.axis_index("los")
    strip = lax.axis_index("sky")
    q = me // 2
    r = me % 2
    last = los // 2 - 1
    partner = me + 1 - 2 * r
    up = (strip + sky - 1) % sky
    down = (strip + 1) % sky

    span = 2 * chunks
    loads = []
    for c in range(span):
        part = (1 - r) if c < chunks else r
        cols = pl.ds(pl.multiple_of((part * chunks + c % chunks) * width, 128), width)
        loads.append(
            pltpu.make_async_copy(pot_hbm.at[:, :, cols], pot.at[:, :, cols], load_sem.at[c])
        )
        loads[-1].start()

    barrier = pltpu.get_barrier_semaphore()
    pl.semaphore_signal(barrier, inc=1, device_id={"los": partner}, device_id_type=MESH)
    pl.semaphore_signal(barrier, inc=1, device_id={"sky": up}, device_id_type=MESH)
    pl.semaphore_signal(barrier, inc=1, device_id={"sky": down}, device_id_type=MESH)

    @pl.when(q > 0)
    def _():
        pl.semaphore_signal(barrier, inc=1, device_id={"los": me - 2}, device_id_type=MESH)

    @pl.when(q < last)
    def _():
        pl.semaphore_signal(barrier, inc=1, device_id={"los": me + 2}, device_id_type=MESH)

    near = [weight_ref[j] * dist_ref[j] for j in range(shells)]
    far = [near[j] * dist_ref[j] for j in range(shells)]
    row = lax.broadcasted_iota(jnp.int32, (8, width), 0)

    def totals(start):
        cols = pl.ds(pl.multiple_of(start, 128), width)
        total_near = jnp.zeros((rows, width), f32)
        total_far = jnp.zeros((rows, width), f32)
        for j in range(shells):
            block = pot[j, :, cols].astype(f32)
            total_near = total_near + near[j] * block
            total_far = total_far + far[j] * block
        return jnp.concatenate([total_near, total_far], axis=0)

    def remote(src, dst, ssem, rsem, **where):
        return pltpu.make_async_remote_copy(
            src_ref=src, dst_ref=dst, send_sem=ssem, recv_sem=rsem,
            device_id=where, device_id_type=MESH,
        )

    x_copies = [
        remote(sent.at[c], got.at[c], x_ssem.at[c], x_rsem.at[c], los=partner)
        for c in range(chunks)
    ] + [remote(sent_rim, got_rim, x_ssem.at[chunks], x_rsem.at[chunks], los=partner)]
    z_copies = [
        remote(onward.at[c], before.at[c], z_ssem.at[c], z_rsem.at[c], los=me + 2)
        for c in range(chunks)
    ] + [remote(onward_rim, before_rim, z_ssem.at[chunks], z_rsem.at[chunks], los=me + 2)]
    b_copies = [
        remote(back.at[c], prefix.at[r, c], b_ssem.at[c], b_rsem.at[c], los=partner)
        for c in range(chunks)
    ] + [remote(back_rim, prefix_rim.at[r], b_ssem.at[chunks], b_rsem.at[chunks], los=partner)]

    edges = [
        remote(edge_send.at[0], edge_recv.at[0], edge_ssem.at[0], edge_rsem.at[0], sky=up),
        remote(edge_send.at[1], edge_recv.at[1], edge_ssem.at[1], edge_rsem.at[1], sky=down),
    ]
    rim_at = max(1, chunks * 5 // 8)

    def send_totals(c):
        sent[c] = totals((1 - r) * half + c * width)
        x_copies[c].start()

    loads[0].wait()
    sent[0] = totals((1 - r) * half)

    peers = 3 + (q > 0).astype(jnp.int32) + (q < last).astype(jnp.int32)
    pl.semaphore_wait(barrier, peers)

    x_copies[0].start()
    for copy in loads[1:]:
        copy.wait()

    for k in range(span):
        cols = pl.ds(k * width, width)
        top = jnp.zeros((8, width), f32)
        bottom = jnp.zeros((8, width), f32)
        for j in range(shells):
            block = pot[j, :, cols].astype(f32)
            mine = (row >= 2 * j) & (row < 2 * j + 2)
            head = block[:8]
            tail = block[rows - 8 :]
            top = jnp.where(mine, pltpu.roll(head, (2 * j) % 8, 0), top)
            bottom = jnp.where(mine, pltpu.roll(tail, (2 * j + 2) % 8, 0), bottom)
        edge_send[0, :, cols] = top.astype(jnp.bfloat16)
        edge_send[1, :, cols] = bottom.astype(jnp.bfloat16)

    for copy in edges:
        copy.start()
    for c in range(1, rim_at):
        send_totals(c)
    for c in range(chunks):
        own[c] = totals(r * half + c * width)

    @pl.when(q == 0)
    def _():
        before[...] = jnp.zeros(before.shape, f32)
        before_rim[...] = jnp.zeros(before_rim.shape, f32)

    for copy in edges:
        copy.wait_recv()

    inner = (row >= 2) & (row < 6)
    for k in range(span):
        cols = pl.ds(k * width, width)
        below = edge_recv[0, :, cols].astype(f32)
        above = edge_recv[1, :, cols].astype(f32)
        total = jnp.zeros((8, width), f32)
        for j in range(shells):
            tile = jnp.where(
                row < 2,
                pltpu.roll(below, (8 - 2 * j) % 8, 0),
                jnp.where(
                    row < 4,
                    pltpu.roll(below, (10 - 2 * j) % 8, 0),
                    jnp.where(
                        row < 6,
                        pltpu.roll(above, (12 - 2 * j) % 8, 0),
                        pltpu.roll(above, (14 - 2 * j) % 8, 0),
                    ),
                ),
            )
            scaled = tile * jnp.where(inner, far[j], near[j])
            rim_pot[j, k] = scaled
            total = total + scaled
        own_rim[k // chunks, k % chunks] = total
    sent_rim[...] = own_rim[1 - r]
    x_copies[chunks].start()

    for c in range(rim_at, chunks):
        send_totals(c)

    is_odd = r.astype(f32)
    is_even = 1.0 - is_odd

    def forward(c):
        x_copies[c].wait_recv()

        @pl.when(q > 0)
        def _():
            z_copies[c].wait_recv()

        if c < chunks:
            mine, other, base = own[c], got[c], before[c]
            next_ref, back_ref, keep_ref = onward.at[c], back.at[c], prefix.at[r, c]
        else:
            mine, other, base = own_rim[r], got_rim[...], before_rim[...]
            next_ref, back_ref, keep_ref = onward_rim, back_rim, prefix_rim.at[r]
        next_ref[...] = base + (mine + other)

        @pl.when(q < last)
        def _():
            z_copies[c].start()

        back_ref[...] = base + is_even * mine
        b_copies[c].start()
        keep_ref[...] = base + is_odd * other

    inverse = [1.0 / jnp.full((8, width), source_ref[j], f32) for j in range(shells)]

    def lens_chunk(place, carry):
        k = (r * chunks + place) % span
        cols = pl.ds(pl.multiple_of(k * width, 128), width)
        part, c = k // chunks, k % chunks
        sums = prefix[part, c]
        run_near, run_far = sums[:rows], sums[rows:]
        rim = prefix_rim[part, c]
        for j in range(shells):
            block = pot[j, :, cols].astype(f32)
            run_near = run_near + near[j] * block
            run_far = run_far + far[j] * block
            rim = rim + rim_pot[j, k]
            far_rim = jnp.where(row < 4, pltpu.roll(rim, 6, 0), pltpu.roll(rim, 2, 0))
            scale = jnp.concatenate([inverse[j]] * (rows // 8), axis=0)
            lens[j, k, :rows] = run_near - run_far * scale
            lens[j, k, rows:] = rim - far_rim * inverse[j]
        return carry

    def stencil_chunk(place, carry):
        k = (r * chunks + place) % span
        cols = pl.ds(pl.multiple_of(k * width, 128), width)
        before_k = (k + span - 1) % span
        after_k = (k + 1) % span
        for j in range(shells):
            centre = lens[j, k]
            wide = jnp.concatenate(
                [lens[j, before_k, :, width - 128 :], centre, lens[j, after_k, :, :128]], axis=1
            )
            full = width + 256

            def shift(n):
                return pltpu.roll(wide, n % full, 1)[:, 128 : 128 + width]

            left1, right1, left2, right2 = shift(1), shift(-1), shift(2), shift(-2)
            slope = (left2 - right2) + 8.0 * (right1 - left1)
            second_x = (16.0 * (left1 + right1) - (left2 + right2))[:rows]

            def rows_at(field, n):
                return pltpu.roll(field, (-n) % (rows + 8), 0)[:rows]

            second_y = 16.0 * (rows_at(centre, -1) + rows_at(centre, 1)) - (
                rows_at(centre, -2) + rows_at(centre, 2)
            )
            cross = (rows_at(slope, -2) - rows_at(slope, 2)) + 8.0 * (
                rows_at(slope, 1) - rows_at(slope, -1)
            )
            middle = 60.0 * centre[:rows]
            conv_ref[j, :, cols] = ((second_x + second_y - middle) * (1.0 / 24.0)).astype(jnp.bfloat16)
            one_ref[j, :, cols] = ((second_x - second_y) * (1.0 / 24.0)).astype(jnp.bfloat16)
            two_ref[j, :, cols] = (cross * (1.0 / 144.0)).astype(jnp.bfloat16)
        return carry

    order = list(range(rim_at)) + [chunks] + list(range(rim_at, chunks))

    @pl.when(q < last)
    def _():
        for c in order:
            forward(c)
        lax.fori_loop(0, chunks, lens_chunk, 0)
        lax.fori_loop(1, chunks - 1, stencil_chunk, 0)
        for c in order:
            b_copies[c].wait_recv()
        lax.fori_loop(chunks, span, lens_chunk, 0)
        lax.fori_loop(chunks - 1, span + 1, stencil_chunk, 0)

    @pl.when(q == last)
    def _():
        arrived, mapped, done = set(), set(), set()

        def run(body, places):
            while places:
                count = 1
                while count < len(places) and places[count] == places[0] + count:
                    count += 1
                lax.fori_loop(places[0], places[0] + count, body, 0)
                places = places[count:]

        def advance(limit):
            ready = []
            for place in sorted(arrived - mapped):
                rim_place = "own" if place < chunks else "other"
                if rim_place in rims:
                    ready.append(place)
            run(lens_chunk, ready)
            mapped.update(ready)
            ready = [
                place
                for place in range(span)
                if place not in done
                and {(place - 1) % span, place, (place + 1) % span} <= mapped
            ][:limit]
            run(stencil_chunk, ready)
            done.update(ready)

        rims = set()

        def receive(c):
            b_copies[c].wait_recv()
            if c == chunks:
                rims.add("other")
            else:
                arrived.add(chunks + c)

        waited = 0
        for n, c in enumerate(order):
            forward(c)
            if c == chunks:
                rims.add("own")
            else:
                arrived.add(c)
            if "own" in rims and n > rim_at:
                while waited < n - 1:
                    receive(order[waited])
                    waited += 1
            advance(4)
        for c in order[waited:]:
            receive(c)
            advance(span)

    for copy in edges:
        copy.wait_send()
    for c in range(chunks + 1):
        x_copies[c].wait_send()
        b_copies[c].wait_send()

    @pl.when(q < last)
    def _():
        for c in range(chunks + 1):
            z_copies[c].wait_send()


def store_kernel(a, b, c, to_a, to_b, to_c, sems):
    copies = [
        pltpu.make_async_copy(src.at[j], dst.at[j], sems.at[n, j])
        for n, (src, dst) in enumerate(((a, to_a), (b, to_b), (c, to_c)))
        for j in range(a.shape[0])
    ]
    for copy in copies:
        copy.start()
    for copy in copies:
        copy.wait()


def on_device(los, sky, potentials, shell_weight, shell_dist, source_dist):
    shells, rows, ncols = potentials.shape
    half = ncols // 2
    chunks = next(n for n in (4, 2, 1) if half % (n * 128) == 0)
    width = half // chunks
    f32, bf16 = jnp.float32, jnp.bfloat16
    dma = pltpu.SemaphoreType.DMA
    smem = pl.BlockSpec(memory_space=pltpu.SMEM)
    vmem = pl.BlockSpec(memory_space=pltpu.VMEM)
    main = (chunks, 2 * rows, width)
    rim = (chunks, 8, width)
    staged = pl.pallas_call(
        functools.partial(lens_kernel, los, sky, chunks, width),
        out_shape=[pltpu.VMEM(potentials.shape, bf16)] * 3,
        in_specs=[smem, smem, smem, pl.BlockSpec(memory_space=pl.ANY)],
        out_specs=[vmem] * 3,
        scratch_shapes=[
            pltpu.VMEM(potentials.shape, bf16),
            pltpu.VMEM((2, 8, ncols), bf16),
            pltpu.VMEM((2, 8, ncols), bf16),
            pltpu.VMEM(main, f32),
            pltpu.VMEM(main, f32),
            pltpu.VMEM(main, f32),
            pltpu.VMEM(rim, f32),
            pltpu.VMEM((2,) + rim, f32),
            pltpu.VMEM(rim, f32),
            pltpu.VMEM(main, f32),
            pltpu.VMEM(rim, f32),
            pltpu.VMEM(main, f32),
            pltpu.VMEM(rim, f32),
            pltpu.VMEM(main, f32),
            pltpu.VMEM(rim, f32),
            pltpu.VMEM((2,) + main, f32),
            pltpu.VMEM((2,) + rim, f32),
            pltpu.VMEM((shells, 2 * chunks, 8, width), f32),
            pltpu.VMEM((shells, 2 * chunks, rows + 8, width), f32),
            dma((2 * chunks,)),
            dma((2,)),
            dma((2,)),
            dma((chunks + 1,)),
            dma((chunks + 1,)),
            dma((chunks + 1,)),
            dma((chunks + 1,)),
            dma((chunks + 1,)),
            dma((chunks + 1,)),
        ],
        compiler_params=pltpu.CompilerParams(collective_id=0, has_side_effects=True),
    )(shell_weight, shell_dist, source_dist, potentials)
    anywhere = pl.BlockSpec(memory_space=pl.ANY)
    return tuple(pl.pallas_call(
        store_kernel,
        out_shape=[jax.ShapeDtypeStruct(potentials.shape, bf16)] * 3,
        in_specs=[vmem] * 3,
        out_specs=[anywhere] * 3,
        scratch_shapes=[dma((3, shells))],
    )(*[pltpu.with_memory_space_constraint(x, pltpu.VMEM) for x in staged]))


def solution(mesh):
    return jax.shard_map(
        functools.partial(on_device, mesh.shape["los"], mesh.shape["sky"]),
        mesh=mesh,
        in_specs=(P("los", "sky", None), P("los"), P("los"), P("los")),
        out_specs=(P("los", "sky", None), P("los", "sky", None), P("los", "sky", None)),
        check_vma=False,
    )
```
